128 devices in a mesh: grid: 16 (over z_lo, y, core), pts: 8 (over x, z_hi).
Axes of the slice: x: 4, y: 4, z: 4 (z_hi: 2, z_lo: 2; z = z_hi * 2 + z_lo), core: 2. Of those that a mesh axis runs over, the one named last changes fastest.
Arguments:
- orbitals: bfloat16 [32768, 512], P(('grid', 'pts')), may hold values from -6 to 6
- point_rows: int32 [128, 8, 24], P(('grid', 'pts')), may hold values from 0 to 255, as said below
- point_count: int32 [128, 8], P(('grid', 'pts')), may hold values from 12 to 24, as said below
- potential: bfloat16 [24576, 8, 3072], P('pts', None, 'grid'), may hold values from -0.0016860962 to 0.0016860962
- fitted_basis: bfloat16 [32768, 24576], P('grid', 'pts'), may hold values from -0.0390625 to 0.0390625
Outputs:
- updated: bfloat16 [32768, 512], P(('grid', 'pts'))
- projection: bfloat16 [24576, 512], P('pts')
The draws below stay inside these ranges and needn't reach their ends.
Inputs may be any that keep to these rules, and one draw needn't show every extreme that they name: `point_count`: each source device has at least one owner with all 24 slots valid. `point_rows`: the listed rows of one source device are all different.
All inputs are finite; a program needn't handle non-finite values.
Results may differ from the reference program's by a relative error of at most 0.0055.
Values may be sent and summed in bfloat16 or wider, within the bound.
No kernel may reach another device: no remote copies, remote signals or barrier semaphores. Data moves between devices by JAX's collectives and lax.ppermute only.
A program may use at most 128 MiB of HBM per device.

```python
import jax
import jax.numpy as jnp
from jax import lax

B = 512
ROWS = 256
CAP = 24
OWN = 3072
M = 24576
NG = 32768
N_GRID = 16
N_PTS = 8


def draw_point_count(key, part):
    first_key, second_key = jax.random.split(jax.random.fold_in(key, 7))
    base_count = jax.random.randint(first_key, (N_GRID * N_PTS, N_PTS), (CAP + 1) // 2, CAP + 1)
    full_owner = jax.random.randint(second_key, (N_GRID * N_PTS, 1), 0, N_PTS)
    owner_ids = jnp.arange(N_PTS, dtype=jnp.int32)[None, :]
    return jnp.where(owner_ids == full_owner, CAP, base_count).astype(jnp.int32)


def draw_point_rows(key, part):
    device_keys = jax.random.split(jax.random.fold_in(key, 11), N_GRID * N_PTS)
    shuffled = jax.vmap(lambda one_key: jax.random.permutation(one_key, ROWS))(device_keys)
    listed = shuffled[:, :N_PTS * CAP]
    return listed.reshape(N_GRID * N_PTS, N_PTS, CAP).astype(jnp.int32)


def levels(key, extent, cuts, least, high):
    gain, own = 1.0, jax.random.fold_in(key, 6)
    for position, parts in cuts:
        steps = jnp.exp(jax.random.uniform(jax.random.fold_in(own, position), (parts,), jnp.float32, least / len(cuts), high / len(cuts)))
        gain = gain * jnp.repeat(steps, extent[position] // parts).reshape([-1 if axis == position else 1 for axis in range(len(extent))])
    return gain


def bell_draw(key, dims, deviation, most, shards=(), held_as=jnp.bfloat16):
    result = jax.random.normal(key, dims, jnp.float32) * deviation
    if len(shards) > 0:
        result = levels(key, dims, shards, -0.22, 0.18) * result
    return jnp.clip(result, min=-most, max=most).astype(held_as)


def setup_inputs(seed: int = 0) -> dict:
    key_list = jax.random.split(jax.random.key(seed), 6)
    orbitals = bell_draw(key_list[0], (NG, B), 1.0, 6.0, ((0, 128),))
    point_rows = draw_point_rows(jax.random.fold_in(key_list[5], 71), 0)
    point_count = draw_point_count(jax.random.fold_in(key_list[5], 71), 0)
    potential = bell_draw(key_list[3], (M, N_PTS, OWN), (1.0 / (B * M) ** 0.5), 0.0016860962, ((0, 8), (2, 16)))
    fitted_basis = bell_draw(key_list[4], (NG, M), M ** -0.5, 0.0390625, ((0, 16), (1, 8)))
    return dict(orbitals=orbitals, point_rows=point_rows, point_count=point_count, potential=potential, fitted_basis=fitted_basis)


def reference(orbitals, point_rows, point_count, potential, fitted_basis):
    devs, owners, per_owner = point_rows.shape
    rows_dev = orbitals.shape[0] // devs
    width = orbitals.shape[1]
    base_rows = (jnp.arange(devs, dtype=jnp.int32) * rows_dev)[:, None, None]
    picked = jnp.take(orbitals, (base_rows + point_rows).astype(jnp.int32), axis=0)
    valid_slot = jnp.arange(per_owner, dtype=jnp.int32)[None, None, :] < point_count[:, :, None]
    picked = jnp.where(valid_slot[..., None], picked, jnp.zeros_like(picked))
    points = jnp.transpose(picked, (1, 0, 2, 3)).reshape(owners * devs * per_owner, width)
    total_slots = points.shape[0]
    own_slots = devs * per_owner
    pot_blocks = potential.reshape(owners, own_slots, total_slots)
    pts_blocks = points.reshape(owners, own_slots, width)

    def block_term(pair_args):
        pot_rows, pts_rows = pair_args
        pair_dens = jnp.dot(pts_rows, points.T, preferred_element_type=jnp.float32)
        weighted = (pot_rows.astype(jnp.float32) * pair_dens).astype(jnp.bfloat16)
        return jnp.dot(weighted, points, preferred_element_type=jnp.float32)

    proj_full = lax.map(block_term, (pot_blocks, pts_blocks))
    projection = proj_full.reshape(total_slots, width).astype(jnp.bfloat16)
    exchange = jnp.dot(fitted_basis, projection, preferred_element_type=jnp.float32)
    updated = (orbitals.astype(jnp.float32) - exchange).astype(jnp.bfloat16)
    return updated, projection
```

```python
import functools

import jax
import jax.numpy as jnp
from jax import lax
from jax.experimental import pallas as pl
from jax.experimental.pallas import tpu as pltpu
from jax.sharding import PartitionSpec as P

BF = jnp.bfloat16
F32 = jnp.float32
B = 512
SUB = 192
CH = 384
COLS = 1536
NY = 4
NX = 4


def grid_perm(zl=0, y=0, c=0):
    pairs = []
    for i in range(16):
        a, r = divmod(i, 8)
        b, d = divmod(r, 2)
        pairs.append((i, (((a + zl) % 2) * 4 + (b + y) % 4) * 2 + (d + c) % 2))
    return pairs


def pts_perm(x=0, zh=0):
    pairs = []
    for i in range(8):
        a, b = divmod(i, 2)
        pairs.append((i, ((a + x) % 4) * 2 + (b + zh) % 2))
    return pairs


def gmove(v, **shift):
    return lax.ppermute(v, "grid", grid_perm(**shift))


def pmove(v, **shift):
    return lax.ppermute(v, "pts", pts_perm(**shift))


def pair_body(n, meta_ref, piece_ref, pot_ref, *refs):
    mine, other = refs[: 2 * n], refs[2 * n : 4 * n]
    send_ref, keep_ref, buf, sems = refs[4 * n :]
    core, same = meta_ref[0], meta_ref[1]

    def fetch(j):
        start = pl.multiple_of(meta_ref[2 + j] * CH, 128)
        return pltpu.make_async_copy(pot_ref.at[:, pl.ds(start, CH)], buf.at[j], sems.at[j])

    for j in range(2 * n):
        fetch(j).start()
    is0 = core == 0
    for j in range(2 * n):
        k, keep = j % n, j >= n
        pick_own = (same == 1) if keep else (same == 0)
        m = jnp.where(pick_own, mine[2 * k][...], mine[2 * k + 1][...])
        o = jnp.where(pick_own, other[2 * k][...], other[2 * k + 1][...])
        rows = jnp.concatenate([jnp.where(is0, m, o), jnp.where(is0, o, m)], axis=0)
        dens = lax.dot_general(
            piece_ref[...], rows, (((1,), (1,)), ((), ())), preferred_element_type=F32
        )
        fetch(j).wait()
        w = (buf[j].astype(F32) * dens).astype(BF)
        out = lax.dot_general(
            w, piece_ref[...], (((0,), (0,)), ((), ())), preferred_element_type=F32
        )
        if keep:
            keep_ref[k] = out
        else:
            send_ref[k] = out.astype(BF)


def pair_call(n, meta, piece, pot_t, mine, other):
    vm = pl.BlockSpec(memory_space=pltpu.VMEM)
    flops = 2 * n * CH * COLS * B * 4
    return pl.pallas_call(
        functools.partial(pair_body, n),
        out_shape=(
            jax.ShapeDtypeStruct((n, CH, B), BF),
            jax.ShapeDtypeStruct((n, CH, B), F32),
        ),
        in_specs=[pl.BlockSpec(memory_space=pltpu.SMEM), vm, pl.BlockSpec(memory_space=pl.ANY)]
        + [vm] * (4 * n),
        out_specs=(vm, vm),
        scratch_shapes=[
            pltpu.VMEM((2 * n, COLS, CH), BF),
            pltpu.SemaphoreType.DMA((2 * n,)),
        ],
        compiler_params=pltpu.CompilerParams(vmem_limit_bytes=28 << 20),
        cost_estimate=pl.CostEstimate(
            flops=flops, bytes_accessed=2 * n * COLS * CH * 2, transcendentals=0
        ),
        name="pair%d" % n,
    )(meta, piece, pot_t, *mine, *other)


def exch_body(n, has_acc, meta_ref, *refs):
    fbs, ts = refs[:n], refs[n : 2 * n]
    acc = refs[2 * n][...] if has_acc else None
    out_ref = refs[-1]
    for fb, t in zip(fbs, ts):
        d = jnp.dot(fb[...], t[...], preferred_element_type=F32)
        acc = d if acc is None else acc + d
    out_ref[...] = acc.astype(out_ref.dtype)


def exch_call(meta, fb, ts, acc, dtype, rt=512):
    n = len(ts)
    tiles = 2048 // rt
    in_specs = [
        pl.BlockSpec((rt, CH), functools.partial(lambda j, i, m: (m[i], m[tiles + j]), j))
        for j in range(n)
    ]
    in_specs += [pl.BlockSpec(memory_space=pltpu.VMEM)] * n
    args = [fb] * n + list(ts)
    if acc is not None:
        in_specs.append(pl.BlockSpec((rt, B), lambda i, m: (m[i], 0)))
        args.append(acc)
    return pl.pallas_call(
        functools.partial(exch_body, n, acc is not None),
        grid_spec=pltpu.PrefetchScalarGridSpec(
            num_scalar_prefetch=1,
            grid=(tiles,),
            in_specs=in_specs,
            out_specs=pl.BlockSpec((rt, B), lambda i, m: (i, 0)),
        ),
        out_shape=jax.ShapeDtypeStruct((2048, B), dtype),
        compiler_params=pltpu.CompilerParams(vmem_limit_bytes=28 << 20),
        cost_estimate=pl.CostEstimate(
            flops=2 * 2048 * CH * n * B, bytes_accessed=2048 * CH * n * 2, transcendentals=0
        ),
        name="exch%d" % n,
    )(meta, *args)


def cat(pred, a, b):
    return jnp.where(pred, jnp.concatenate([a, b], 0), jnp.concatenate([b, a], 0))


def on_device(orbitals, point_rows, point_count, potential, fitted_basis):
    g, p = lax.axis_index("grid"), lax.axis_index("pts")
    zl, y, c = g // 8, (g // 2) % NY, g % 2
    x, zh = p // 2, p % 2
    i32 = jnp.int32

    valid = lax.broadcasted_iota(i32, (8, 24), 1) < point_count[0][:, None]
    index = jnp.where(valid, point_rows[0], -1).reshape(SUB, 1)
    pick = (index == lax.broadcasted_iota(i32, (SUB, 256), 1)).astype(BF)
    picked = jnp.dot(pick, orbitals, preferred_element_type=F32).astype(BF)

    slot = lax.all_to_all(picked.reshape(8, 24, B), "pts", 0, 0, tiled=True).reshape(SUB, B)

    zpart = pmove(picked, zh=1)
    both = cat(zh == 0, picked[None], zpart[None]).reshape(2, 8, 24, B)
    xa = pmove(both, x=1)
    xb = pmove(both, x=-1)
    x2 = jnp.stack([pmove(xa[0], x=1), pmove(xb[1], x=-1)])
    piece = jnp.zeros((8, NX, 2, 24, B), BF)
    for v, s in ((both, 0), (xa, -1), (xb, 1), (x2, 2)):
        piece = lax.dynamic_update_slice(
            piece, v.transpose(1, 0, 2, 3)[:, None], (0, (x + s) % NX, 0, 0, 0)
        )
    piece = piece.reshape(COLS, B)

    rz = gmove(slot, zl=1)
    mine0 = jnp.stack([slot, rz])
    part0 = gmove(mine0, c=1)
    blk_a = gmove(mine0, y=1)
    blk_b = gmove(mine0, y=-1)
    part_a = gmove(blk_a, c=1)
    part_b = gmove(blk_b, c=1)
    far_0 = gmove(blk_a[0], y=1)
    far_1 = gmove(blk_b[1], y=-1)
    far = jnp.stack([far_0, far_1])
    part_f = gmove(far, c=1)

    pot_t = jnp.transpose(potential, (1, 2, 0)).reshape(COLS, 8 * CH)
    same = (zl == c).astype(i32)
    head = [c, same]

    def meta(shifts):
        return jnp.stack(
            head
            + [(1 - c) * NY + (y + s) % NY for s in shifts]
            + [c * NY + (y + s) % NY for s in shifts]
        ).astype(i32)

    send0, keep0 = pair_call(
        1, meta([0]), piece, pot_t, [mine0[0], mine0[1]], [part0[0], part0[1]]
    )
    k0 = (keep0[0] + gmove(send0, c=1)[0].astype(F32)).astype(BF)
    ya = gmove(k0[:SUB], y=1)
    yb = gmove(k0[SUB:], y=-1)
    send1, keep1 = pair_call(
        2, meta([-1, 1]), piece, pot_t,
        [blk_a[0], blk_a[1], blk_b[0], blk_b[1]],
        [part_a[0], part_a[1], part_b[0], part_b[1]],
    )
    k1 = keep1 + gmove(send1, c=1).astype(F32)
    to_a = jnp.concatenate([k1[0, :SUB] + ya.astype(F32), k1[0, SUB:]], 0).astype(BF)
    to_b = jnp.concatenate([k1[1, :SUB], k1[1, SUB:] + yb.astype(F32)], 0).astype(BF)
    ra = gmove(to_a, y=1)
    rb = gmove(to_b, y=-1)
    send2, keep2 = pair_call(
        1, meta([2]), piece, pot_t, [far[0], far[1]], [part_f[0], part_f[1]]
    )
    total = keep2[0] + gmove(send2, c=1)[0].astype(F32) + ra.astype(F32) + rb.astype(F32)
    lo, hi = total[:SUB], total[SUB:]
    zs = gmove(jnp.where(zl == 0, hi, lo).astype(BF), zl=1)
    proj_own = (jnp.where(zl == 0, lo, hi) + zs.astype(F32)).astype(BF)

    t0 = cat(zl == 0, proj_own, gmove(proj_own, zl=1))
    ta = gmove(t0, y=1)
    tb = gmove(t0, y=-1)
    t2 = jnp.concatenate([gmove(ta[:SUB], y=1), gmove(tb[SUB:], y=-1)], 0)
    q0, qa, qb, q2 = [gmove(t, c=1) for t in (t0, ta, tb, t2)]
    d = 1 - c
    col = lambda core, s: core * NY + (y + s) % NY
    ident = [jnp.int32(i) for i in range(4)]
    acc = exch_call(
        jnp.stack(ident + [col(c, 2), col(d, 2)]).astype(i32), fitted_basis, [t0, q0], None, F32
    )
    acc = exch_call(
        jnp.stack(ident + [col(c, 1), col(d, 1), col(c, 3), col(d, 3)]).astype(i32),
        fitted_basis, [ta, qa, tb, qb], acc, F32,
    )
    order = [(x + s) % NX for s in (2, 1, -1, 0)]
    part = exch_call(
        jnp.stack(order + [col(c, 0), col(d, 0)]).astype(i32), fitted_basis, [t2, q2], acc, F32
    )
    projection = jnp.zeros((8, CH, B), BF)
    for t, core, s in (
        (t0, c, 2), (q0, d, 2), (ta, c, 1), (qa, d, 1), (tb, c, 3), (qb, d, 3), (t2, c, 0), (q2, d, 0)
    ):
        projection = lax.dynamic_update_slice(projection, t[None], (col(core, s), 0, 0))
    projection = projection.reshape(8 * CH, B)

    part = part.reshape(NX, 2, 256, B)
    xa = pmove(part[0, 0].astype(BF), x=1)
    xb = pmove(part[0, 1].astype(BF), x=-1)
    to_a = jnp.stack([part[1, 0] + xa.astype(F32), part[1, 1]]).astype(BF)
    to_b = jnp.stack([part[2, 0], part[2, 1] + xb.astype(F32)]).astype(BF)
    total = part[3] + pmove(to_a, x=1).astype(F32) + pmove(to_b, x=-1).astype(F32)
    zs = pmove(jnp.where(zh == 0, total[1], total[0]).astype(BF), zh=1)
    exchange = jnp.where(zh == 0, total[0], total[1]) + zs.astype(F32)
    updated = (orbitals.astype(F32) - exchange).astype(BF)
    return (updated, projection)


def solution(mesh):
    in_specs = (
        P(("grid", "pts"), None),
        P(("grid", "pts"), None, None),
        P(("grid", "pts"), None),
        P("pts", None, "grid"),
        P("grid", "pts"),
    )
    out_specs = (P(("grid", "pts"), None), P("pts", None))
    return jax.shard_map(
        on_device, mesh=mesh, in_specs=in_specs, out_specs=out_specs, check_vma=False
    )
```

```python
import functools

import jax
import jax.numpy as jnp
from jax import lax
from jax.experimental import pallas as pl
from jax.experimental.pallas import tpu as pltpu
from jax.sharding import PartitionSpec as P


BF = jnp.bfloat16
F32 = jnp.float32
B = 512
SUB = 192
CH = 384
COLS = 1536
NY = 4
NX = 4
RT = 512
HB = 256


def grid_perm(zl=0, y=0, c=0):
    pairs = []
    for i in range(16):
        a, r = divmod(i, 8)
        b, d = divmod(r, 2)
        pairs.append((i, (((a + zl) % 2) * 4 + (b + y) % 4) * 2 + (d + c) % 2))
    return pairs


def pts_perm(x=0, zh=0):
    pairs = []
    for i in range(8):
        a, b = divmod(i, 2)
        pairs.append((i, ((a + x) % 4) * 2 + (b + zh) % 2))
    return pairs


def gmove(v, **shift):
    return lax.ppermute(v, "grid", grid_perm(**shift))


def pmove(v, **shift):
    return lax.ppermute(v, "pts", pts_perm(**shift))


def pick_body(rows_ref, count_ref, orb_ref, out_ref):
    lane = lax.broadcasted_iota(jnp.int32, (1, 24), 1)
    row = lax.broadcasted_iota(jnp.int32, (256, 24), 0)
    parts = []
    for q in range(8):
        index = jnp.where(lane < count_ref[0, q], rows_ref[0, q : q + 1, :], -1)
        parts.append((row == index).astype(BF))
    pick = jnp.concatenate(parts, axis=1)
    out_ref[...] = lax.dot_general(
        pick, orb_ref[...], (((0,), (0,)), ((), ())), preferred_element_type=F32
    ).astype(BF)


def pick_call(rows, count, orbitals):
    vm = pl.BlockSpec(memory_space=pltpu.VMEM)
    return pl.pallas_call(
        pick_body,
        out_shape=jax.ShapeDtypeStruct((SUB, B), BF),
        in_specs=[vm, pl.BlockSpec(memory_space=pltpu.SMEM), vm],
        out_specs=vm,
        name="pick",
    )(rows, count, orbitals)


def pair_body(n, kind, picks, meta_ref, piece_ref, pot_ref, *refs):
    count = 1 + max(i for block in picks for i, _ in block)
    arrays, rest = refs[:count], refs[count:]
    buf, sems = rest[-2:]
    core, same = meta_ref[0], meta_ref[1]

    def fetch(j):
        start = pl.multiple_of(meta_ref[2 + j] * CH, 128)
        return pltpu.make_async_copy(pot_ref.at[:, pl.ds(start, CH)], buf.at[j], sems.at[j])

    for j in range(n):
        fetch(j).start()
    is0 = core == 0
    pick_own = (same == 0) if kind == "send" else (same == 1)
    for j in range(n):
        near_m, far_m, near_o, far_o = [
            arrays[i][...] if at is None else arrays[i][at] for i, at in picks[j]
        ]
        m = jnp.where(pick_own, near_m, far_m)
        o = jnp.where(pick_own, near_o, far_o)
        rows = jnp.concatenate([jnp.where(is0, m, o), jnp.where(is0, o, m)], axis=0)
        dens = lax.dot_general(
            piece_ref[...], rows, (((1,), (1,)), ((), ())), preferred_element_type=F32
        )
        fetch(j).wait()
        w = (buf[j].astype(F32) * dens).astype(BF)
        out = lax.dot_general(
            w, piece_ref[...], (((0,), (0,)), ((), ())), preferred_element_type=F32
        )
        if kind == "send":
            rest[0][j] = out.astype(BF)
        elif kind == "keep":
            rest[0][...] = out
        elif kind == "first":
            got, top, low = rest[:3]
            out = (out + got[0].astype(F32)).astype(BF)
            top[...] = out[:SUB]
            low[...] = out[SUB:]
        else:
            got, near, o_ref = rest[0], rest[1 + j], rest[3 + j]
            out = out + got[j].astype(F32)
            add = near[...].astype(F32)
            top, low = (out[:SUB] + add, out[SUB:]) if j == 0 else (out[:SUB], out[SUB:] + add)
            o_ref[:SUB, :] = top.astype(BF)
            o_ref[SUB:, :] = low.astype(BF)


def pair_call(kind, meta, piece, pot_t, arrays, picks, extra=()):
    n = len(picks)
    vm = pl.BlockSpec(memory_space=pltpu.VMEM)
    shape = jax.ShapeDtypeStruct
    outs = {
        "send": [shape((n, CH, B), BF)],
        "keep": [shape((CH, B), F32)],
        "first": [shape((SUB, B), BF)] * 2,
        "second": [shape((CH, B), BF)] * 2,
    }[kind]
    return pl.pallas_call(
        functools.partial(pair_body, n, kind, picks),
        out_shape=outs,
        in_specs=[
            pl.BlockSpec(memory_space=pltpu.SMEM), vm, pl.BlockSpec(memory_space=pltpu.HBM)
        ] + [vm] * (len(arrays) + len(extra)),
        out_specs=[vm] * len(outs),
        scratch_shapes=[pltpu.VMEM((n, COLS, CH), BF), pltpu.SemaphoreType.DMA((n,))],
        compiler_params=pltpu.CompilerParams(vmem_limit_bytes=9 << 20),
        cost_estimate=pl.CostEstimate(
            flops=2 * n * CH * COLS * B * 2,
            bytes_accessed=n * COLS * CH * 2,
            transcendentals=0,
        ),
    )(meta, piece, pot_t, *arrays, *extra)


def exch_body(n, kind, places, meta_ref, fb_ref, *refs):
    ts, rest = refs[:n], refs[n:]
    k = sum(r.shape[0] for r in ts) // CH
    if kind == "first":
        out_ref, proj_ref, buf, sems, proj_sems, part, out_sems = rest
    elif kind == "next":
        acc_ref, _, out_ref, proj_ref, buf, sems, proj_sems, part, out_sems, acc, acc_sems = rest
    else:
        acc_ref, _, *x_sends, x_own, z_send, z_own, proj_ref, buf, sems, proj_sems, acc, acc_sems = rest

    def fetch(i, j):
        row = pl.multiple_of(meta_ref[1 + i] * RT, RT)
        start = pl.multiple_of(meta_ref[5 + j] * CH, 128)
        return pltpu.make_async_copy(
            fb_ref.at[pl.ds(row, RT), pl.ds(start, CH)],
            buf.at[i, :, pl.ds(j * CH, CH)],
            sems.at[i, j],
        )

    def before(i):
        row = pl.multiple_of(meta_ref[1 + i] * RT, RT)
        return pltpu.make_async_copy(acc_ref.at[pl.ds(row, RT)], acc.at[i], acc_sems.at[i])

    def store(i):
        return pltpu.make_async_copy(part.at[i], out_ref.at[pl.ds(i * RT, RT)], out_sems.at[i])

    def place(j):
        block, at = places[j]
        row = pl.multiple_of(meta_ref[5 + block] * CH + at, SUB)
        return pltpu.make_async_copy(
            ts[j], proj_ref.at[pl.ds(row, ts[j].shape[0])], proj_sems.at[j]
        )

    def begin(i):
        for j in range(k):
            fetch(i, j).start()
        if kind != "first":
            before(i).start()

    begin(0)
    begin(1)
    t = jnp.concatenate([r[...] for r in ts], axis=0)
    zh = meta_ref[0]
    for i in range(4):
        for j in range(k):
            fetch(i, j).wait()
        if i < 2:
            begin(i + 2)
        if i == 1:
            for j in range(n):
                place(j).start()
        d = jnp.dot(buf[i], t, preferred_element_type=F32)
        if kind != "first":
            before(i).wait()
            d = d + acc[i]
        if kind != "last":
            part[i] = d
            store(i).start()
            continue
        if i < 3:
            x_sends[i][...] = d[:, :HB].astype(BF)
        else:
            x_own[...] = d[:, :HB]
        lo, hi = d[:256, HB:], d[256:, HB:]
        z_send[i] = jnp.where(zh == 0, hi, lo).astype(BF)
        z_own[i] = jnp.where(zh == 0, lo, hi)
    if kind != "last":
        for i in range(4):
            store(i).wait()
    for j in range(n):
        place(j).wait()


def exch_call(kind, zh, order, cols, fb, ts, acc=None, proj=None):
    n, k = len(ts), len(cols)
    vm = pl.BlockSpec(memory_space=pltpu.VMEM)
    hbm = pl.BlockSpec(memory_space=pltpu.HBM)
    shape = jax.ShapeDtypeStruct
    tile = pltpu.VMEM((4, RT, B), F32)
    dma = pltpu.SemaphoreType.DMA
    scratch = [pltpu.VMEM((4, RT, k * CH), BF), dma((4, k)), dma((n,))]
    if kind != "last":
        scratch += [tile, dma((4,))]
    if kind != "first":
        scratch += [tile, dma((4,))]
    outs, out_specs = [pltpu.HBM((4 * RT, B), F32)], [hbm]
    if kind == "last":
        outs = [shape((RT, HB), BF)] * 3 + [
            shape((RT, HB), F32), shape((4, 256, HB), BF), shape((4, 256, HB), F32)
        ]
        out_specs = [vm] * len(outs)
    outs, out_specs = outs + [pltpu.HBM((8 * CH, B), BF)], out_specs + [hbm]
    places, row = [], 0
    for t in ts:
        places.append((row // CH, row % CH))
        row += t.shape[0]
    args = [] if acc is None else [acc, proj]
    args = [pltpu.with_memory_space_constraint(v, pltpu.HBM) for v in args]
    return pl.pallas_call(
        functools.partial(exch_body, n, kind, places),
        out_shape=outs,
        in_specs=[pl.BlockSpec(memory_space=pltpu.SMEM), hbm] + [vm] * n + [hbm] * len(args),
        out_specs=out_specs,
        input_output_aliases={} if acc is None else {3 + n: len(outs) - 1},
        scratch_shapes=scratch,
        compiler_params=pltpu.CompilerParams(
            vmem_limit_bytes={"first": 11, "next": 21, "last": 13}[kind] << 20
        ),
        cost_estimate=pl.CostEstimate(
            flops=2 * 4 * RT * CH * k * B,
            bytes_accessed=4 * RT * CH * k * 2,
            transcendentals=0,
        ),
    )(jnp.stack([zh] + order + cols).astype(jnp.int32), fb, *ts, *args)


def small_call(body, outs, *args, smem=0, aliases=None):
    vm = pl.BlockSpec(memory_space=pltpu.VMEM)
    return pl.pallas_call(
        body,
        out_shape=outs,
        in_specs=[pl.BlockSpec(memory_space=pltpu.SMEM)] * smem + [vm] * (len(args) - smem),
        out_specs=[vm] * len(outs),
        input_output_aliases=aliases or {},
        compiler_params=pltpu.CompilerParams(vmem_limit_bytes=6 << 20),
    )(*args)


def piece_body(blocks, at_ref, *refs):
    out_ref = refs[-1]
    for i in range(blocks):
        for q in range(8):
            out_ref[q, at_ref[2 * i], at_ref[2 * i + 1]] = refs[i][q]


def cut_body(rows_a, rows_b, a_ref, b_ref, a_out, b_out):
    a_out[...] = a_ref[rows_a]
    b_out[...] = b_ref[rows_b]


def zsum_body(own_ref, got_ref, *outs):
    for i in range(4):
        outs[i][...] = (own_ref[i] + got_ref[i].astype(F32)).astype(outs[i].dtype)


def step(orbitals, point_rows, point_count, potential, fitted_basis):
    g, p = lax.axis_index("grid"), lax.axis_index("pts")
    zl, y, c = g // 8, (g // 2) % NY, g % 2
    x, zh = p // 2, p % 2
    i32 = jnp.int32
    fitted_basis = pltpu.with_memory_space_constraint(fitted_basis, pltpu.HBM)

    picked = pick_call(point_rows, point_count, orbitals)
    xa0 = pmove(picked, x=1)
    xb0 = pmove(picked, x=-1)
    zpart = pmove(picked, zh=1)
    xa1 = pmove(zpart, x=1)
    xb1 = pmove(zpart, x=-1)
    x2a = pmove(xa0, x=1)
    x2b = pmove(xb1, x=-1)
    spots = []
    for v, s, at in (
        (picked, 0, zh), (zpart, 0, 1 - zh), (xa0, -1, zh), (xa1, -1, 1 - zh),
        (xb0, 1, zh), (xb1, 1, 1 - zh), (x2a, 2, zh), (x2b, 2, 1 - zh),
    ):
        spots.append((v.reshape(8, 24, B), (x + s) % NX, at))
    shape = jax.ShapeDtypeStruct((8, NX, 2, 24, B), BF)
    for name, some in (("k_piece1", spots[:6]), ("k_piece2", spots[6:])):
        at = jnp.stack([i for _, a, b in some for i in (a, b)]).astype(i32)
        args = [v for v, _, _ in some]
        if name == "k_piece2":
            args.append(piece)
        (piece,) = small_call(
            functools.partial(piece_body, len(some)), [shape], at, *args,
            smem=1, aliases={len(args): 0} if name == "k_piece2" else None,
        )
    piece = piece.reshape(COLS, B)

    slot = lax.all_to_all(picked.reshape(8, 24, B), "pts", 0, 0, tiled=True)
    slot = slot.reshape(SUB, B)
    rz = gmove(slot, zl=1)
    mine0 = jnp.stack([slot, rz])
    part0 = gmove(mine0, c=1)
    blk_a = gmove(mine0, y=1)
    blk_b = gmove(mine0, y=-1)
    part_a = gmove(blk_a, c=1)
    part_b = gmove(blk_b, c=1)
    rows = jax.ShapeDtypeStruct((SUB, B), BF)
    cut_a, cut_b = small_call(functools.partial(cut_body, 0, 1), [rows, rows], blk_a, blk_b)
    far_0 = gmove(cut_a, y=1)
    far_1 = gmove(cut_b, y=-1)
    part_0 = gmove(far_0, c=1)
    part_1 = gmove(far_1, c=1)

    pot_t = jnp.transpose(potential, (1, 2, 0)).reshape(COLS, 8 * CH)
    pot_t = pltpu.with_memory_space_constraint(pot_t, pltpu.HBM)
    same = (zl == c).astype(i32)

    def pairs(kind, shifts, arrays, picks, extra=()):
        core = 1 - c if kind == "send" else c
        meta = jnp.stack([c, same] + [core * NY + (y + s) % NY for s in shifts]).astype(i32)
        return pair_call(kind, meta, piece, pot_t, arrays, picks, extra)

    rows0 = [mine0, part0], [[(0, 0), (0, 1), (1, 0), (1, 1)]]
    rows1 = [blk_a, blk_b, part_a, part_b], [
        [(k, 0), (k, 1), (2 + k, 0), (2 + k, 1)] for k in range(2)
    ]
    rows2 = [far_0, far_1, part_0, part_1], [[(k, None) for k in range(4)]]
    (send0,) = pairs("send", [0], *rows0)
    got0 = gmove(send0, c=1)
    top, low = pairs("first", [0], *rows0, (got0,))
    ya = gmove(top, y=1)
    yb = gmove(low, y=-1)
    (send1,) = pairs("send", [-1, 1], *rows1)
    got1 = gmove(send1, c=1)
    to_a, to_b = pairs("second", [-1, 1], *rows1, (got1, ya, yb))
    ra = gmove(to_a, y=1)
    rb = gmove(to_b, y=-1)
    (send2,) = pairs("send", [2], *rows2)
    got2 = gmove(send2, c=1)
    (keep2,) = pairs("keep", [2], *rows2)
    total = keep2 + got2[0].astype(F32) + ra.astype(F32) + rb.astype(F32)
    total = total.astype(BF)
    zs = gmove(total, zl=1)

    t0 = (total.astype(F32) + zs.astype(F32)).astype(BF)
    ta = gmove(t0, y=1)
    tb = gmove(t0, y=-1)
    q0 = gmove(t0, c=1)
    cut_a, cut_b = small_call(
        functools.partial(cut_body, slice(0, SUB), slice(SUB, CH)), [rows, rows], ta, tb
    )
    t2a = gmove(cut_a, y=1)
    t2b = gmove(cut_b, y=-1)
    qa = gmove(ta, c=1)
    qb = gmove(tb, c=1)
    q2a = gmove(t2a, c=1)
    q2b = gmove(t2b, c=1)
    d = 1 - c
    col = lambda core, s: core * NY + (y + s) % NY
    ident = [jnp.int32(i) for i in range(4)]
    acc, proj = exch_call("first", zh, ident, [col(c, 2), col(d, 2)], fitted_basis, [t0, q0])
    cols = [col(c, 1), col(c, 3), col(d, 1), col(d, 3)]
    acc, proj = exch_call("next", zh, ident, cols, fitted_basis, [ta, tb, qa, qb], acc, proj)
    order = [(x + s) % NX for s in (2, 1, -1, 0)]
    x_2, x_1, x_3, x_own, z_send, z_own, projection = exch_call(
        "last", zh, order, [col(c, 0), col(d, 0)], fitted_basis,
        [t2a, t2b, q2a, q2b], acc, proj,
    )

    def over_x(to_2, to_1, to_3, own):
        total = own
        for v, s in ((to_2, 2), (to_1, 1), (to_3, -1)):
            total = total + pmove(v, x=s).astype(F32)
        return total

    z_got = pmove(z_send, zh=1)
    x_sum = over_x(x_2, x_1, x_3, x_own)
    quarter = lambda dtype: jax.ShapeDtypeStruct((256, HB), dtype)
    z_parts = small_call(zsum_body, [quarter(BF)] * 3 + [quarter(F32)], z_own, z_got)
    right = over_x(*z_parts)
    lo, hi = x_sum[:256], x_sum[256:]
    left = jnp.where(zh == 0, lo, hi) + pmove(
        jnp.where(zh == 0, hi, lo).astype(BF), zh=1
    ).astype(F32)
    exchange = jnp.concatenate([left, right], axis=1)
    updated = (orbitals.astype(F32) - exchange).astype(BF)
    return (updated, projection)


def solution(mesh):
    in_specs = (
        P(("grid", "pts"), None),
        P(("grid", "pts"), None, None),
        P(("grid", "pts"), None),
        P("pts", None, "grid"),
        P("grid", "pts"),
    )
    out_specs = (P(("grid", "pts"), None), P("pts", None))
    return jax.shard_map(step, mesh=mesh, in_specs=in_specs, out_specs=out_specs, check_vma=False)
```

```python
import functools

import jax
import jax.numpy as jnp
from jax import lax
from jax.experimental import pallas as pl
from jax.experimental.pallas import tpu as pltpu
from jax.sharding import PartitionSpec as P


BF = jnp.bfloat16
F32 = jnp.float32
B = 512
SUB = 192
CH = 384
COLS = 1536
NY = 4
NX = 4
RT = 512
HB = 256


def grid_perm(zl=0, y=0, c=0):
    pairs = []
    for i in range(16):
        a, r = divmod(i, 8)
        b, d = divmod(r, 2)
        pairs.append((i, (((a + zl) % 2) * 4 + (b + y) % 4) * 2 + (d + c) % 2))
    return pairs


def pts_perm(x=0, zh=0):
    pairs = []
    for i in range(8):
        a, b = divmod(i, 2)
        pairs.append((i, ((a + x) % 4) * 2 + (b + zh) % 2))
    return pairs


def gmove(v, **shift):
    return lax.ppermute(v, "grid", grid_perm(**shift))


def pmove(v, **shift):
    return lax.ppermute(v, "pts", pts_perm(**shift))


def pick_body(rows_ref, count_ref, orb_ref, out_ref):
    lane = lax.broadcasted_iota(jnp.int32, (1, 24), 1)
    row = lax.broadcasted_iota(jnp.int32, (256, 24), 0)
    parts = []
    for q in range(8):
        index = jnp.where(lane < count_ref[0, q], rows_ref[0, q : q + 1, :], -1)
        parts.append((row == index).astype(BF))
    pick = jnp.concatenate(parts, axis=1)
    out_ref[...] = lax.dot_general(
        pick, orb_ref[...], (((0,), (0,)), ((), ())), preferred_element_type=F32
    ).astype(BF)


def pick_call(rows, count, orbitals):
    vm = pl.BlockSpec(memory_space=pltpu.VMEM)
    return pl.pallas_call(
        pick_body,
        out_shape=jax.ShapeDtypeStruct((SUB, B), BF),
        in_specs=[vm, pl.BlockSpec(memory_space=pltpu.SMEM), vm],
        out_specs=vm,
        name="pick",
    )(rows, count, orbitals)


def pair_body(n, kind, picks, meta_ref, piece_ref, pot_ref, *refs):
    count = 1 + max(i for block in picks for i, _ in block)
    arrays, rest = refs[:count], refs[count:]
    buf, sems = rest[-2:]
    core, same = meta_ref[0], meta_ref[1]

    def fetch(j):
        start = pl.multiple_of(meta_ref[2 + j] * CH, 128)
        return pltpu.make_async_copy(pot_ref.at[:, pl.ds(start, CH)], buf.at[j], sems.at[j])

    for j in range(n):
        fetch(j).start()
    is0 = core == 0
    pick_own = (same == 0) if kind == "send" else (same == 1)
    for j in range(n):
        near_m, far_m, near_o, far_o = [
            arrays[i][...] if at is None else arrays[i][at] for i, at in picks[j]
        ]
        m = jnp.where(pick_own, near_m, far_m)
        o = jnp.where(pick_own, near_o, far_o)
        rows = jnp.concatenate([jnp.where(is0, m, o), jnp.where(is0, o, m)], axis=0)
        dens = lax.dot_general(
            piece_ref[...], rows, (((1,), (1,)), ((), ())), preferred_element_type=F32
        )
        fetch(j).wait()
        w = (buf[j].astype(F32) * dens).astype(BF)
        out = lax.dot_general(
            w, piece_ref[...], (((0,), (0,)), ((), ())), preferred_element_type=F32
        )
        if kind == "send":
            rest[0][j] = out.astype(BF)
        elif kind == "keep":
            rest[0][...] = out
        elif kind == "first":
            got, top, low = rest[:3]
            out = (out + got[0].astype(F32)).astype(BF)
            top[...] = out[:SUB]
            low[...] = out[SUB:]
        else:
            got, near, o_ref = rest[0], rest[1 + j], rest[3 + j]
            out = out + got[j].astype(F32)
            add = near[...].astype(F32)
            top, low = (out[:SUB] + add, out[SUB:]) if j == 0 else (out[:SUB], out[SUB:] + add)
            o_ref[:SUB, :] = top.astype(BF)
            o_ref[SUB:, :] = low.astype(BF)


def pair_call(kind, meta, piece, pot_t, arrays, picks, extra=()):
    n = len(picks)
    vm = pl.BlockSpec(memory_space=pltpu.VMEM)
    shape = jax.ShapeDtypeStruct
    outs = {
        "send": [shape((n, CH, B), BF)],
        "keep": [shape((CH, B), F32)],
        "first": [shape((SUB, B), BF)] * 2,
        "second": [shape((CH, B), BF)] * 2,
    }[kind]
    return pl.pallas_call(
        functools.partial(pair_body, n, kind, picks),
        out_shape=outs,
        in_specs=[
            pl.BlockSpec(memory_space=pltpu.SMEM), vm, pl.BlockSpec(memory_space=pltpu.HBM)
        ] + [vm] * (len(arrays) + len(extra)),
        out_specs=[vm] * len(outs),
        scratch_shapes=[pltpu.VMEM((n, COLS, CH), BF), pltpu.SemaphoreType.DMA((n,))],
        compiler_params=pltpu.CompilerParams(vmem_limit_bytes=9 << 20),
        cost_estimate=pl.CostEstimate(
            flops=2 * n * CH * COLS * B * 2,
            bytes_accessed=n * COLS * CH * 2,
            transcendentals=0,
        ),
    )(meta, piece, pot_t, *arrays, *extra)


def exch_body(n, kind, meta_ref, fb_ref, *refs):
    ts, rest = refs[:n], refs[n:]
    if kind == "first":
        out_ref, proj_ref, buf, sems, proj_sems, part, out_sems = rest
    elif kind == "next":
        acc_ref, _, out_ref, proj_ref, buf, sems, proj_sems, part, out_sems, acc, acc_sems = rest
    else:
        acc_ref, _, *x_sends, x_own, z_send, z_own, proj_ref, buf, sems, proj_sems, acc, acc_sems = rest

    def fetch(i, j):
        row = pl.multiple_of(meta_ref[1 + i] * RT, RT)
        start = pl.multiple_of(meta_ref[5 + j] * CH, 128)
        return pltpu.make_async_copy(
            fb_ref.at[pl.ds(row, RT), pl.ds(start, CH)],
            buf.at[i, :, pl.ds(j * CH, CH)],
            sems.at[i, j],
        )

    def before(i):
        row = pl.multiple_of(meta_ref[1 + i] * RT, RT)
        return pltpu.make_async_copy(acc_ref.at[pl.ds(row, RT)], acc.at[i], acc_sems.at[i])

    def store(i):
        return pltpu.make_async_copy(part.at[i], out_ref.at[pl.ds(i * RT, RT)], out_sems.at[i])

    def place(j):
        row = pl.multiple_of(meta_ref[5 + j] * CH, CH)
        return pltpu.make_async_copy(ts[j], proj_ref.at[pl.ds(row, CH)], proj_sems.at[j])

    def begin(i):
        for j in range(n):
            fetch(i, j).start()
        if kind != "first":
            before(i).start()

    begin(0)
    begin(1)
    t = jnp.concatenate([r[...] for r in ts], axis=0)
    zh = meta_ref[0]
    for i in range(4):
        for j in range(n):
            fetch(i, j).wait()
        if i < 2:
            begin(i + 2)
        if i == 1:
            for j in range(n):
                place(j).start()
        d = jnp.dot(buf[i], t, preferred_element_type=F32)
        if kind != "first":
            before(i).wait()
            d = d + acc[i].astype(F32)
        if kind != "last":
            part[i] = d.astype(BF)
            store(i).start()
            continue
        if i < 3:
            x_sends[i][...] = d[:, :HB].astype(BF)
        else:
            x_own[...] = d[:, :HB]
        lo, hi = d[:256, HB:], d[256:, HB:]
        z_send[i] = jnp.where(zh == 0, hi, lo).astype(BF)
        z_own[i] = jnp.where(zh == 0, lo, hi)
    if kind != "last":
        for i in range(4):
            store(i).wait()
    for j in range(n):
        place(j).wait()


def exch_call(kind, zh, order, cols, fb, ts, acc=None, proj=None):
    n = len(ts)
    vm = pl.BlockSpec(memory_space=pltpu.VMEM)
    hbm = pl.BlockSpec(memory_space=pltpu.HBM)
    shape = jax.ShapeDtypeStruct
    tile = pltpu.VMEM((4, RT, B), BF)
    dma = pltpu.SemaphoreType.DMA
    scratch = [pltpu.VMEM((4, RT, n * CH), BF), dma((4, n)), dma((n,))]
    if kind != "last":
        scratch += [tile, dma((4,))]
    if kind != "first":
        scratch += [tile, dma((4,))]
    outs, out_specs = [pltpu.HBM((4 * RT, B), BF)], [hbm]
    if kind == "last":
        outs = [shape((RT, HB), BF)] * 3 + [
            shape((RT, HB), F32), shape((4, 256, HB), BF), shape((4, 256, HB), F32)
        ]
        out_specs = [vm] * len(outs)
    outs, out_specs = outs + [pltpu.HBM((8 * CH, B), BF)], out_specs + [hbm]
    args = [] if acc is None else [acc, proj]
    args = [pltpu.with_memory_space_constraint(v, pltpu.HBM) for v in args]
    return pl.pallas_call(
        functools.partial(exch_body, n, kind),
        out_shape=outs,
        in_specs=[pl.BlockSpec(memory_space=pltpu.SMEM), hbm] + [vm] * n + [hbm] * len(args),
        out_specs=out_specs,
        input_output_aliases={} if acc is None else {3 + n: len(outs) - 1},
        scratch_shapes=scratch,
        compiler_params=pltpu.CompilerParams(
            vmem_limit_bytes={"first": 11, "next": 21, "last": 13}[kind] << 20
        ),
        cost_estimate=pl.CostEstimate(
            flops=2 * 4 * RT * CH * n * B,
            bytes_accessed=4 * RT * CH * n * 2,
            transcendentals=0,
        ),
    )(jnp.stack([zh] + order + cols).astype(jnp.int32), fb, *ts, *args)


def small_call(body, outs, *args, smem=0, aliases=None):
    vm = pl.BlockSpec(memory_space=pltpu.VMEM)
    return pl.pallas_call(
        body,
        out_shape=outs,
        in_specs=[pl.BlockSpec(memory_space=pltpu.SMEM)] * smem + [vm] * (len(args) - smem),
        out_specs=[vm] * len(outs),
        input_output_aliases=aliases or {},
        compiler_params=pltpu.CompilerParams(vmem_limit_bytes=6 << 20),
    )(*args)


def piece_body(blocks, at_ref, *refs):
    out_ref = refs[-1]
    for i in range(blocks):
        for q in range(8):
            out_ref[q, at_ref[2 * i], at_ref[2 * i + 1]] = refs[i][q]


def cut_body(a_ref, b_ref, a_out, b_out):
    a_out[...] = a_ref[0]
    b_out[...] = b_ref[1]


def xsum_body(zh_ref, own_ref, got_2, got_1, got_3, send_ref, keep_ref):
    total = own_ref[...]
    for got in (got_2, got_1, got_3):
        total = total + got[...].astype(F32)
    lo, hi = total[:256], total[256:]
    first = zh_ref[0] == 0
    send_ref[...] = jnp.where(first, hi, lo).astype(BF)
    keep_ref[...] = jnp.where(first, lo, hi)


def last_body(orb_ref, left_ref, left_got, own_ref, got_2, got_1, got_3, out_ref):
    left = left_ref[...] + left_got[...].astype(F32)
    out_ref[:, :HB] = (orb_ref[:, :HB].astype(F32) - left).astype(BF)
    right = own_ref[...]
    for got in (got_2, got_1, got_3):
        right = right + got[...].astype(F32)
    out_ref[:, HB:] = (orb_ref[:, HB:].astype(F32) - right).astype(BF)


def zsum_body(own_ref, got_ref, *outs):
    for i in range(4):
        outs[i][...] = (own_ref[i] + got_ref[i].astype(F32)).astype(outs[i].dtype)


def step(orbitals, point_rows, point_count, potential, fitted_basis):
    g, p = lax.axis_index("grid"), lax.axis_index("pts")
    zl, y, c = g // 8, (g // 2) % NY, g % 2
    x, zh = p // 2, p % 2
    i32 = jnp.int32
    fitted_basis = pltpu.with_memory_space_constraint(fitted_basis, pltpu.HBM)

    picked = pick_call(point_rows, point_count, orbitals)
    xa0 = pmove(picked, x=1)
    xb0 = pmove(picked, x=-1)
    zpart = pmove(picked, zh=1)
    xa1 = pmove(zpart, x=1)
    xb1 = pmove(zpart, x=-1)
    x2a = pmove(xa0, x=1)
    x2b = pmove(xb1, x=-1)
    spots = []
    for v, s, at in (
        (picked, 0, zh), (zpart, 0, 1 - zh), (xa0, -1, zh), (xa1, -1, 1 - zh),
        (xb0, 1, zh), (xb1, 1, 1 - zh), (x2a, 2, zh), (x2b, 2, 1 - zh),
    ):
        spots.append((v.reshape(8, 24, B), (x + s) % NX, at))
    shape = jax.ShapeDtypeStruct((8, NX, 2, 24, B), BF)
    for name, some in (("k_piece1", spots[:6]), ("k_piece2", spots[6:])):
        at = jnp.stack([i for _, a, b in some for i in (a, b)]).astype(i32)
        args = [v for v, _, _ in some]
        if name == "k_piece2":
            args.append(piece)
        (piece,) = small_call(
            functools.partial(piece_body, len(some)), [shape], at, *args,
            smem=1, aliases={len(args): 0} if name == "k_piece2" else None,
        )
    piece = piece.reshape(COLS, B)

    slot = lax.all_to_all(picked.reshape(8, 24, B), "pts", 0, 0, tiled=True)
    slot = slot.reshape(SUB, B)
    rz = gmove(slot, zl=1)
    mine0 = jnp.stack([slot, rz])
    part0 = gmove(mine0, c=1)
    blk_a = gmove(mine0, y=1)
    blk_b = gmove(mine0, y=-1)
    part_a = gmove(blk_a, c=1)
    part_b = gmove(blk_b, c=1)
    rows = jax.ShapeDtypeStruct((SUB, B), BF)
    cut_a, cut_b = small_call(cut_body, [rows, rows], blk_a, blk_b)
    far_0 = gmove(cut_a, y=1)
    far_1 = gmove(cut_b, y=-1)
    part_0 = gmove(far_0, c=1)
    part_1 = gmove(far_1, c=1)

    pot_t = jnp.transpose(potential, (1, 2, 0)).reshape(COLS, 8 * CH)
    pot_t = pltpu.with_memory_space_constraint(pot_t, pltpu.HBM)
    same = (zl == c).astype(i32)

    def pairs(kind, shifts, arrays, picks, extra=()):
        core = 1 - c if kind == "send" else c
        meta = jnp.stack([c, same] + [core * NY + (y + s) % NY for s in shifts]).astype(i32)
        return pair_call(kind, meta, piece, pot_t, arrays, picks, extra)

    rows0 = [mine0, part0], [[(0, 0), (0, 1), (1, 0), (1, 1)]]
    rows1 = [blk_a, blk_b, part_a, part_b], [
        [(k, 0), (k, 1), (2 + k, 0), (2 + k, 1)] for k in range(2)
    ]
    rows2 = [far_0, far_1, part_0, part_1], [[(k, None) for k in range(4)]]
    (send0,) = pairs("send", [0], *rows0)
    got0 = gmove(send0, c=1)
    top, low = pairs("first", [0], *rows0, (got0,))
    ya = gmove(top, y=1)
    yb = gmove(low, y=-1)
    (send1,) = pairs("send", [-1, 1], *rows1)
    got1 = gmove(send1, c=1)
    to_a, to_b = pairs("second", [-1, 1], *rows1, (got1, ya, yb))
    ra = gmove(to_a, y=1)
    rb = gmove(to_b, y=-1)
    (send2,) = pairs("send", [2], *rows2)
    got2 = gmove(send2, c=1)
    (keep2,) = pairs("keep", [2], *rows2)
    total = keep2 + got2[0].astype(F32) + ra.astype(F32) + rb.astype(F32)
    total = total.astype(BF)
    zs = gmove(total, zl=1)

    t0 = (total.astype(F32) + zs.astype(F32)).astype(BF)
    ta = gmove(t0, y=1)
    tb = gmove(t0, y=-1)
    q0 = gmove(t0, c=1)
    t2 = gmove(t0, y=2)
    qa = gmove(ta, c=1)
    qb = gmove(tb, c=1)
    q2 = gmove(t2, c=1)
    d = 1 - c
    col = lambda core, s: core * NY + (y + s) % NY
    ident = [jnp.int32(i) for i in range(4)]
    acc, proj = exch_call("first", zh, ident, [col(c, 2), col(d, 2)], fitted_basis, [t0, q0])
    cols = [col(c, 1), col(c, 3), col(d, 1), col(d, 3)]
    acc, proj = exch_call("next", zh, ident, cols, fitted_basis, [ta, tb, qa, qb], acc, proj)
    order = [(x + s) % NX for s in (2, 1, -1, 0)]
    x_2, x_1, x_3, x_own, z_send, z_own, projection = exch_call(
        "last", zh, order, [col(c, 0), col(d, 0)], fitted_basis,
        [t2, q2], acc, proj,
    )

    def over_x(*sent):
        return [pmove(v, x=s) for v, s in zip(sent, (2, 1, -1))]

    z_got = pmove(z_send, zh=1)
    x_got = over_x(x_2, x_1, x_3)
    quarter = lambda dtype: jax.ShapeDtypeStruct((256, HB), dtype)
    z_2, z_1, z_3, right = small_call(zsum_body, [quarter(BF)] * 3 + [quarter(F32)], z_own, z_got)
    right_got = over_x(z_2, z_1, z_3)
    x_send, left = small_call(
        xsum_body, [quarter(BF), quarter(F32)], zh.reshape(1), x_own, *x_got, smem=1
    )
    left_got = pmove(x_send, zh=1)
    (updated,) = small_call(
        last_body, [jax.ShapeDtypeStruct((256, B), BF)],
        orbitals, left, left_got, right, *right_got,
    )
    return (updated, projection)


def solution(mesh):
    in_specs = (
        P(("grid", "pts"), None),
        P(("grid", "pts"), None, None),
        P(("grid", "pts"), None),
        P("pts", None, "grid"),
        P("grid", "pts"),
    )
    out_specs = (P(("grid", "pts"), None), P("pts", None))
    return jax.shard_map(step, mesh=mesh, in_specs=in_specs, out_specs=out_specs, check_vma=False)
```

```python
import functools

import jax
import jax.numpy as jnp
from jax import lax
from jax.experimental import pallas as pl
from jax.experimental.pallas import tpu as pltpu
from jax.sharding import PartitionSpec as P


BF = jnp.bfloat16
F32 = jnp.float32
B = 512
SUB = 192
CH = 384
COLS = 1536
NY = 4
NX = 4
RT = 512
HB = 256


def grid_perm(zl=0, y=0, c=0):
    pairs = []
    for i in range(16):
        a, r = divmod(i, 8)
        b, d = divmod(r, 2)
        pairs.append((i, (((a + zl) % 2) * 4 + (b + y) % 4) * 2 + (d + c) % 2))
    return pairs


def pts_perm(x=0, zh=0):
    pairs = []
    for i in range(8):
        a, b = divmod(i, 2)
        pairs.append((i, ((a + x) % 4) * 2 + (b + zh) % 2))
    return pairs


def gmove(v, **shift):
    return lax.ppermute(v, "grid", grid_perm(**shift))


def pmove(v, **shift):
    return lax.ppermute(v, "pts", pts_perm(**shift))


def pick_body(rows_ref, count_ref, orb_ref, out_ref):
    lane = lax.broadcasted_iota(jnp.int32, (1, 24), 1)
    row = lax.broadcasted_iota(jnp.int32, (256, 24), 0)
    parts = []
    for q in range(8):
        index = jnp.where(lane < count_ref[0, q], rows_ref[0, q : q + 1, :], -1)
        parts.append((row == index).astype(BF))
    pick = jnp.concatenate(parts, axis=1)
    out_ref[...] = lax.dot_general(
        pick, orb_ref[...], (((0,), (0,)), ((), ())), preferred_element_type=F32
    ).astype(BF)


def pick_call(rows, count, orbitals):
    vm = pl.BlockSpec(memory_space=pltpu.VMEM)
    return pl.pallas_call(
        pick_body,
        out_shape=jax.ShapeDtypeStruct((SUB, B), BF),
        in_specs=[vm, pl.BlockSpec(memory_space=pltpu.SMEM), vm],
        out_specs=vm,
        name="pick",
    )(rows, count, orbitals)


def pair_body(n, kind, picks, meta_ref, piece_ref, pot_ref, *refs):
    count = 1 + max(i for block in picks for i, _ in block)
    arrays, rest = refs[:count], refs[count:]
    buf, sems = rest[-2:]
    core, same = meta_ref[0], meta_ref[1]

    def fetch(j):
        start = pl.multiple_of(meta_ref[2 + j] * CH, 128)
        return pltpu.make_async_copy(pot_ref.at[:, pl.ds(start, CH)], buf.at[j], sems.at[j])

    for j in range(n):
        fetch(j).start()
    is0 = core == 0
    pick_own = (same == 0) if kind == "send" else (same == 1)
    for j in range(n):
        near_m, far_m, near_o, far_o = [
            arrays[i][...] if at is None else arrays[i][at] for i, at in picks[j]
        ]
        m = jnp.where(pick_own, near_m, far_m)
        o = jnp.where(pick_own, near_o, far_o)
        rows = jnp.concatenate([jnp.where(is0, m, o), jnp.where(is0, o, m)], axis=0)
        dens = lax.dot_general(
            piece_ref[...], rows, (((1,), (1,)), ((), ())), preferred_element_type=F32
        )
        fetch(j).wait()
        w = (buf[j].astype(F32) * dens).astype(BF)
        out = lax.dot_general(
            w, piece_ref[...], (((0,), (0,)), ((), ())), preferred_element_type=F32
        )
        if kind == "send":
            rest[0][j] = out.astype(BF)
        elif kind == "keep":
            rest[0][...] = out
        elif kind == "first":
            got, top, low = rest[:3]
            out = (out + got[0].astype(F32)).astype(BF)
            top[...] = out[:SUB]
            low[...] = out[SUB:]
        else:
            got, near, o_ref = rest[0], rest[1 + j], rest[3 + j]
            out = out + got[j].astype(F32)
            add = near[...].astype(F32)
            top, low = (out[:SUB] + add, out[SUB:]) if j == 0 else (out[:SUB], out[SUB:] + add)
            o_ref[:SUB, :] = top.astype(BF)
            o_ref[SUB:, :] = low.astype(BF)


def pair_call(kind, meta, piece, pot_t, arrays, picks, extra=()):
    n = len(picks)
    vm = pl.BlockSpec(memory_space=pltpu.VMEM)
    shape = jax.ShapeDtypeStruct
    outs = {
        "send": [shape((n, CH, B), BF)],
        "keep": [shape((CH, B), F32)],
        "first": [shape((SUB, B), BF)] * 2,
        "second": [shape((CH, B), BF)] * 2,
    }[kind]
    return pl.pallas_call(
        functools.partial(pair_body, n, kind, picks),
        out_shape=outs,
        in_specs=[
            pl.BlockSpec(memory_space=pltpu.SMEM), vm, pl.BlockSpec(memory_space=pltpu.HBM)
        ] + [vm] * (len(arrays) + len(extra)),
        out_specs=[vm] * len(outs),
        scratch_shapes=[pltpu.VMEM((n, COLS, CH), BF), pltpu.SemaphoreType.DMA((n,))],
        compiler_params=pltpu.CompilerParams(vmem_limit_bytes=9 << 20),
        cost_estimate=pl.CostEstimate(
            flops=2 * n * CH * COLS * B * 2,
            bytes_accessed=n * COLS * CH * 2,
            transcendentals=0,
        ),
    )(meta, piece, pot_t, *arrays, *extra)


def exch_body(n, kind, meta_ref, fb_ref, *refs):
    ts, rest = refs[:n], refs[n:]
    if kind == "first":
        out_ref, proj_ref, buf, sems, proj_sems, part, out_sems = rest
    elif kind == "next":
        acc_ref, _, out_ref, proj_ref, buf, sems, proj_sems, part, out_sems, acc, acc_sems = rest
    else:
        acc_ref, _, *x_sends, x_own, z_send, z_own, proj_ref, buf, sems, proj_sems, acc, acc_sems = rest

    def fetch(i, j):
        row = pl.multiple_of(meta_ref[1 + i] * RT, RT)
        start = pl.multiple_of(meta_ref[5 + j] * CH, 128)
        return pltpu.make_async_copy(
            fb_ref.at[pl.ds(row, RT), pl.ds(start, CH)],
            buf.at[i, :, pl.ds(j * CH, CH)],
            sems.at[i, j],
        )

    def before(i):
        row = pl.multiple_of(meta_ref[1 + i] * RT, RT)
        return pltpu.make_async_copy(acc_ref.at[pl.ds(row, RT)], acc.at[i], acc_sems.at[i])

    def store(i):
        return pltpu.make_async_copy(part.at[i], out_ref.at[pl.ds(i * RT, RT)], out_sems.at[i])

    def place(j):
        row = pl.multiple_of(meta_ref[5 + j] * CH, CH)
        return pltpu.make_async_copy(ts[j], proj_ref.at[pl.ds(row, CH)], proj_sems.at[j])

    def begin(i):
        for j in range(n):
            fetch(i, j).start()
        if kind != "first":
            before(i).start()

    begin(0)
    begin(1)
    t = jnp.concatenate([r[...] for r in ts], axis=0)
    zh = meta_ref[0]
    for i in range(4):
        for j in range(n):
            fetch(i, j).wait()
        if i < 2:
            begin(i + 2)
        if i == 1:
            for j in range(n):
                place(j).start()
        d = jnp.dot(buf[i], t, preferred_element_type=F32)
        if kind != "first":
            before(i).wait()
            d = d + acc[i].astype(F32)
        if kind != "last":
            part[i] = d.astype(BF)
            store(i).start()
            continue
        if i < 3:
            x_sends[i][...] = d[:, :HB].astype(BF)
        else:
            x_own[...] = d[:, :HB]
        lo, hi = d[:256, HB:], d[256:, HB:]
        z_send[i] = jnp.where(zh == 0, hi, lo).astype(BF)
        z_own[i] = jnp.where(zh == 0, lo, hi)
    if kind != "last":
        for i in range(4):
            store(i).wait()
    for j in range(n):
        place(j).wait()


def exch_call(kind, zh, order, cols, fb, ts, acc=None, proj=None):
    n = len(ts)
    vm = pl.BlockSpec(memory_space=pltpu.VMEM)
    hbm = pl.BlockSpec(memory_space=pltpu.HBM)
    shape = jax.ShapeDtypeStruct
    tile = pltpu.VMEM((4, RT, B), BF)
    dma = pltpu.SemaphoreType.DMA
    scratch = [pltpu.VMEM((4, RT, n * CH), BF), dma((4, n)), dma((n,))]
    if kind != "last":
        scratch += [tile, dma((4,))]
    if kind != "first":
        scratch += [tile, dma((4,))]
    outs, out_specs = [pltpu.HBM((4 * RT, B), BF)], [hbm]
    if kind == "last":
        outs = [shape((RT, HB), BF)] * 3 + [
            shape((RT, HB), F32), shape((4, 256, HB), BF), shape((4, 256, HB), F32)
        ]
        out_specs = [vm] * len(outs)
    outs, out_specs = outs + [pltpu.HBM((8 * CH, B), BF)], out_specs + [hbm]
    args = [] if acc is None else [acc, proj]
    args = [pltpu.with_memory_space_constraint(v, pltpu.HBM) for v in args]
    return pl.pallas_call(
        functools.partial(exch_body, n, kind),
        out_shape=outs,
        in_specs=[pl.BlockSpec(memory_space=pltpu.SMEM), hbm] + [vm] * n + [hbm] * len(args),
        out_specs=out_specs,
        input_output_aliases={} if acc is None else {3 + n: len(outs) - 1},
        scratch_shapes=scratch,
        compiler_params=pltpu.CompilerParams(
            vmem_limit_bytes={"first": 11, "next": 21, "last": 13}[kind] << 20
        ),
        cost_estimate=pl.CostEstimate(
            flops=2 * 4 * RT * CH * n * B,
            bytes_accessed=4 * RT * CH * n * 2,
            transcendentals=0,
        ),
    )(jnp.stack([zh] + order + cols).astype(jnp.int32), fb, *ts, *args)


def small_call(body, outs, *args, smem=0, aliases=None):
    vm = pl.BlockSpec(memory_space=pltpu.VMEM)
    return pl.pallas_call(
        body,
        out_shape=outs,
        in_specs=[pl.BlockSpec(memory_space=pltpu.SMEM)] * smem + [vm] * (len(args) - smem),
        out_specs=[vm] * len(outs),
        input_output_aliases=aliases or {},
        compiler_params=pltpu.CompilerParams(vmem_limit_bytes=6 << 20),
    )(*args)


def piece_body(blocks, at_ref, *refs):
    out_ref = refs[-1]
    for i in range(blocks):
        for q in range(8):
            out_ref[q, at_ref[2 * i], at_ref[2 * i + 1]] = refs[i][q]


def cut_body(a_ref, b_ref, a_out, b_out):
    a_out[...] = a_ref[0]
    b_out[...] = b_ref[1]


def xsum_body(zh_ref, own_ref, got_2, got_1, got_3, send_ref, keep_ref):
    total = own_ref[...]
    for got in (got_2, got_1, got_3):
        total = total + got[...].astype(F32)
    lo, hi = total[:256], total[256:]
    first = zh_ref[0] == 0
    send_ref[...] = jnp.where(first, hi, lo).astype(BF)
    keep_ref[...] = jnp.where(first, lo, hi)


def last_body(orb_ref, left_ref, left_got, own_ref, got_2, got_1, got_3, out_ref):
    left = left_ref[...] + left_got[...].astype(F32)
    out_ref[:, :HB] = (orb_ref[:, :HB].astype(F32) - left).astype(BF)
    right = own_ref[...]
    for got in (got_2, got_1, got_3):
        right = right + got[...].astype(F32)
    out_ref[:, HB:] = (orb_ref[:, HB:].astype(F32) - right).astype(BF)


def zsum_body(own_ref, got_ref, *outs):
    for i in range(4):
        outs[i][...] = (own_ref[i] + got_ref[i].astype(F32)).astype(outs[i].dtype)


def step(orbitals, point_rows, point_count, potential, fitted_basis):
    g, p = lax.axis_index("grid"), lax.axis_index("pts")
    zl, y, c = g // 8, (g // 2) % NY, g % 2
    x, zh = p // 2, p % 2
    i32 = jnp.int32
    fitted_basis = pltpu.with_memory_space_constraint(fitted_basis, pltpu.HBM)

    picked = pick_call(point_rows, point_count, orbitals)
    xa0 = pmove(picked, x=1)
    xb0 = pmove(picked, x=-1)
    zpart = pmove(picked, zh=1)
    xa1 = pmove(zpart, x=1)
    xb1 = pmove(zpart, x=-1)
    x2a = pmove(xa0, x=1)
    x2b = pmove(xb1, x=-1)
    spots = []
    for v, s, at in (
        (picked, 0, zh), (zpart, 0, 1 - zh), (xa0, -1, zh), (xb0, 1, zh),
        (xa1, -1, 1 - zh), (xb1, 1, 1 - zh), (x2a, 2, zh), (x2b, 2, 1 - zh),
    ):
        spots.append((v.reshape(8, 24, B), (x + s) % NX, at))
    shape = jax.ShapeDtypeStruct((8, NX, 2, 24, B), BF)
    piece = None
    for some in (spots[:4], spots[4:6], spots[6:]):
        at = jnp.stack([i for _, a, b in some for i in (a, b)]).astype(i32)
        args = [v for v, _, _ in some] + ([] if piece is None else [piece])
        aliases = None if piece is None else {len(args): 0}
        (piece,) = small_call(
            functools.partial(piece_body, len(some)), [shape], at, *args,
            smem=1, aliases=aliases,
        )
    piece = piece.reshape(COLS, B)

    slot = lax.all_to_all(picked.reshape(8, 24, B), "pts", 0, 0, tiled=True)
    slot = slot.reshape(SUB, B)
    rz = gmove(slot, zl=1)
    mine0 = jnp.stack([slot, rz])
    part0 = gmove(mine0, c=1)
    blk_a = gmove(mine0, y=1)
    blk_b = gmove(mine0, y=-1)
    part_a = gmove(blk_a, c=1)
    part_b = gmove(blk_b, c=1)
    rows = jax.ShapeDtypeStruct((SUB, B), BF)
    cut_a, cut_b = small_call(cut_body, [rows, rows], blk_a, blk_b)
    far_0 = gmove(cut_a, y=1)
    far_1 = gmove(cut_b, y=-1)
    part_0 = gmove(far_0, c=1)
    part_1 = gmove(far_1, c=1)

    pot_t = jnp.transpose(potential, (1, 2, 0)).reshape(COLS, 8 * CH)
    pot_t = pltpu.with_memory_space_constraint(pot_t, pltpu.HBM)
    same = (zl == c).astype(i32)

    def pairs(kind, shifts, arrays, picks, extra=()):
        core = 1 - c if kind == "send" else c
        meta = jnp.stack([c, same] + [core * NY + (y + s) % NY for s in shifts]).astype(i32)
        return pair_call(kind, meta, piece, pot_t, arrays, picks, extra)

    rows0 = [mine0, part0], [[(0, 0), (0, 1), (1, 0), (1, 1)]]
    rows1 = [blk_a, blk_b, part_a, part_b], [
        [(k, 0), (k, 1), (2 + k, 0), (2 + k, 1)] for k in range(2)
    ]
    rows2 = [far_0, far_1, part_0, part_1], [[(k, None) for k in range(4)]]
    (send0,) = pairs("send", [0], *rows0)
    got0 = gmove(send0, c=1)
    top, low = pairs("first", [0], *rows0, (got0,))
    ya = gmove(top, y=1)
    yb = gmove(low, y=-1)
    (send1,) = pairs("send", [-1, 1], *rows1)
    got1 = gmove(send1, c=1)
    to_a, to_b = pairs("second", [-1, 1], *rows1, (got1, ya, yb))
    ra = gmove(to_a, y=1)
    rb = gmove(to_b, y=-1)
    (send2,) = pairs("send", [2], *rows2)
    got2 = gmove(send2, c=1)
    (keep2,) = pairs("keep", [2], *rows2)
    total = keep2 + got2[0].astype(F32) + ra.astype(F32) + rb.astype(F32)
    total = total.astype(BF)
    zs = gmove(total, zl=1)

    t0 = (total.astype(F32) + zs.astype(F32)).astype(BF)
    ta = gmove(t0, y=1)
    tb = gmove(t0, y=-1)
    q0 = gmove(t0, c=1)
    t2 = jnp.concatenate([gmove(ta[:SUB], y=1), gmove(tb[SUB:], y=-1)], 0)
    qa = gmove(ta, c=1)
    qb = gmove(tb, c=1)
    q2 = gmove(t2, c=1)
    d = 1 - c
    col = lambda core, s: core * NY + (y + s) % NY
    ident = [jnp.int32(i) for i in range(4)]
    acc, proj = exch_call("first", zh, ident, [col(c, 2), col(d, 2)], fitted_basis, [t0, q0])
    cols = [col(c, 1), col(c, 3), col(d, 1), col(d, 3)]
    acc, proj = exch_call("next", zh, ident, cols, fitted_basis, [ta, tb, qa, qb], acc, proj)
    order = [(x + s) % NX for s in (2, 1, -1, 0)]
    x_2, x_1, x_3, x_own, z_send, z_own, projection = exch_call(
        "last", zh, order, [col(c, 0), col(d, 0)], fitted_basis,
        [t2, q2], acc, proj,
    )

    def over_x(*sent):
        return [pmove(v, x=s) for v, s in zip(sent, (2, 1, -1))]

    z_got = pmove(z_send, zh=1)
    x_got = over_x(x_2, x_1, x_3)
    quarter = lambda dtype: jax.ShapeDtypeStruct((256, HB), dtype)
    z_2, z_1, z_3, right = small_call(zsum_body, [quarter(BF)] * 3 + [quarter(F32)], z_own, z_got)
    right_got = over_x(z_2, z_1, z_3)
    x_send, left = small_call(
        xsum_body, [quarter(BF), quarter(F32)], zh.reshape(1), x_own, *x_got, smem=1
    )
    left_got = pmove(x_send, zh=1)
    (updated,) = small_call(
        last_body, [jax.ShapeDtypeStruct((256, B), BF)],
        orbitals, left, left_got, right, *right_got,
    )
    return (updated, projection)


def solution(mesh):
    in_specs = (
        P(("grid", "pts"), None),
        P(("grid", "pts"), None, None),
        P(("grid", "pts"), None),
        P("pts", None, "grid"),
        P("grid", "pts"),
    )
    out_specs = (P(("grid", "pts"), None), P("pts", None))
    return jax.shard_map(step, mesh=mesh, in_specs=in_specs, out_specs=out_specs, check_vma=False)
```
